128 devices in a mesh: src: 16 (over z, x_hi, core), dst: 8 (over x_lo, y).
Axes of the slice: x: 4 (x_hi: 2, x_lo: 2; x = x_hi * 2 + x_lo), y: 4, z: 4, core: 2. Of those that a mesh axis runs over, the one named last changes fastest.
Arguments:
- adjacency: float32 [20480, 20480], P('dst', 'src'), may hold values from -0.0625 to 0.0625
- features: float32 [20480, 256], P(('src', 'dst')), may hold values from -6 to 6
- layer_weights: float32 [2, 2, 256, 256], replicated, may hold values from -0.375 to 0.375
- layer_biases: float32 [2, 256], replicated, may hold values from -3 to 3
Outputs:
- result: float32 [20480, 256], P(('src', 'dst'))
The draws below stay inside these ranges and needn't reach their ends.
All inputs are finite; a program needn't handle non-finite values.
Results may differ from the reference program's by a relative error of at most 0.0001.
Values sent between devices are 32-bit elements; how exact they have to be, the bound alone decides.
No kernel may reach another device: no remote copies, remote signals or barrier semaphores. Data moves between devices by JAX's collectives and lax.ppermute only.
A program may use at most 128 MiB of HBM per device.

```python
import jax
import jax.numpy as jnp
from jax import lax

F = 256
LAYERS = 2
NODES = 20480


def strengthened(array, key, source, target, shards_of, factor):
    owner, partner = [(jnp.arange(array.shape[position]) // (array.shape[position] // shards_of)).reshape([-1 if axis == position else 1 for axis in range(array.ndim)]) for position in (source, target)]
    chosen = jax.random.permutation(key, shards_of)[partner]
    strong = (owner == chosen) | (owner == (partner + shards_of // 2) % shards_of)
    return jnp.where(strong, factor * array, array)


def level_of(key, extent, split, low, high):
    gain = 1.0
    for axis_at, shards_of in split:
        heights = jax.random.uniform(jax.random.fold_in(jax.random.fold_in(key, 6), axis_at), (shards_of,), jnp.float32, low / len(split), high / len(split))
        gain = gain * jnp.repeat(jnp.exp(heights), extent[axis_at] // shards_of).reshape((-1,) + (1,) * (len(extent) - 1 - axis_at))
    return gain


def normal_values(own_key, extent, scale, reach, pieces=(), dtype=jnp.bfloat16):
    factor_of = level_of(own_key, extent, pieces, -0.22, 0.18) if pieces else 1.0
    entries = jax.random.normal(own_key, extent, jnp.float32) * scale * factor_of
    return jnp.minimum(jnp.maximum(entries, -reach), reach).astype(dtype)


def heavy_noise(own_key, dims, width, bound, split, heavy, dtype=jnp.bfloat16):
    drawn = width * jax.random.normal(own_key, dims, jnp.float32)
    if split:
        drawn = drawn * level_of(own_key, dims, split, -0.22, 0.18)
    return jnp.clip(strengthened(drawn, jax.random.fold_in(own_key, 3), *heavy), -bound, bound).astype(dtype)


def setup_inputs(seed: int = 0) -> dict:
    splits = jax.random.split(jax.random.key(seed), 5)
    return {
        "adjacency": heavy_noise(splits[0], (NODES, NODES), NODES ** -0.5, 0.0625, ((0, 8), (1, 16)), (1, 0, 16, 2.0), jnp.float32),
        "features": normal_values(splits[1], (NODES, F), 1.0, 6.0, ((0, 128),), jnp.float32),
        "layer_weights": normal_values(splits[2], (LAYERS, 2, F, F), F ** -0.5, 0.375, (), jnp.float32),
        "layer_biases": normal_values(splits[3], (LAYERS, F), 0.5, 3.0, (), jnp.float32),
    }


def reference(adjacency, features, layer_weights, layer_biases):
    current = features
    for layer_index in range(LAYERS):
        forward = jnp.dot(adjacency, current, precision=lax.Precision.HIGHEST, preferred_element_type=jnp.float32)
        reverse = lax.dot_general(adjacency, current, (((0,), (0,)), ((), ())), precision=lax.Precision.HIGHEST, preferred_element_type=jnp.float32)
        mixed = jnp.dot(forward, layer_weights[layer_index, 0], precision=lax.Precision.HIGHEST, preferred_element_type=jnp.float32)
        mixed = mixed + jnp.dot(reverse, layer_weights[layer_index, 1], precision=lax.Precision.HIGHEST, preferred_element_type=jnp.float32)
        current = jax.nn.relu(mixed + layer_biases[layer_index][None, :])
    return current
```

```python
import itertools

import jax
import jax.numpy as jnp
from jax import lax
from jax.sharding import Mesh
from jax.sharding import PartitionSpec as P

LAYERS = 2

SRC = ("z", "xh", "core")
DST = ("xl", "y")
CHIP = ("z", "xh")
SIZE = {"z": 4, "xh": 2, "core": 2, "xl": 2, "y": 4}
PARTS = 8


def rotation(axes, steps):
    pairs = []
    for place in itertools.product(*(range(SIZE[a]) for a in axes)):
        source = target = 0
        for axis, at, step in zip(axes, place, steps):
            source = source * SIZE[axis] + at
            target = target * SIZE[axis] + (at + step) % SIZE[axis]
        pairs.append((source, target))
    return pairs


def shifted(axes, steps, sign):
    index = 0
    for axis, step in zip(axes, steps):
        index = index * SIZE[axis] + lax.rem(
            lax.axis_index(axis) + sign * step + SIZE[axis], SIZE[axis]
        )
    return index


def all_steps(axes):
    return [s for s in itertools.product(*(range(SIZE[a]) for a in axes)) if any(s)]


def gather(block, axes):
    rows = block.shape[0]
    whole = jnp.zeros((PARTS * rows, block.shape[1]), block.dtype)
    nowhere = (0,) * len(axes)
    whole = lax.dynamic_update_slice(whole, block, (shifted(axes, nowhere, 1) * rows, 0))
    for steps in all_steps(axes):
        got = lax.ppermute(block, axes, rotation(axes, steps))
        whole = lax.dynamic_update_slice(whole, got, (shifted(axes, steps, -1) * rows, 0))
    return whole


def scatter_sum(parts, axes):
    rows = parts.shape[0] // PARTS
    nowhere = (0,) * len(axes)
    share = lambda steps: lax.dynamic_slice_in_dim(parts, shifted(axes, steps, 1) * rows, rows, 0)
    total = share(nowhere)
    for steps in all_steps(axes):
        total = total + lax.ppermute(share(steps), axes, rotation(axes, steps))
    return total


def exchange_cores(value):
    return lax.ppermute(value, "core", [(0, 1), (1, 0)])


def turn(value):
    pairs = []
    for chip, core, dst in itertools.product(range(PARTS), range(2), range(PARTS)):
        pairs.append(((chip * 2 + core) * PARTS + dst, (dst * 2 + core) * PARTS + chip))
    return lax.ppermute(value, SRC + DST, pairs)


def split(value):
    high = lax.reduce_precision(value, 8, 7)
    return high.astype(jnp.bfloat16), (value - high).astype(jnp.bfloat16)


def product(left, right, dims):
    dot = lambda a, b: lax.dot_general(a, b, (dims, ((), ())), preferred_element_type=jnp.float32)
    return dot(left[0], right[0]) + dot(left[0], right[1]) + dot(left[1], right[0])


def mix(forward, reverse, weights, bias):
    dot = lambda a, b: jnp.dot(
        a, b, precision=lax.Precision.HIGHEST, preferred_element_type=jnp.float32
    )
    return jax.nn.relu(dot(forward, weights[0]) + dot(reverse, weights[1]) + bias[None, :])


def body(adjacency, features, layer_weights, layer_biases):
    core = lax.axis_index("core")
    half = adjacency.shape[0] // 2
    own = split(lax.dynamic_slice_in_dim(adjacency, core * half, half, 0))
    other = split(lax.dynamic_slice_in_dim(adjacency, (1 - core) * half, half, 0))
    row_block = features
    column_block = turn(features)
    for layer in range(LAYERS):
        source_rows = split(gather(row_block, DST))
        own_rows = gather(column_block, CHIP)
        other_rows = split(exchange_cores(own_rows))
        own_rows = split(own_rows)
        sent = product(other, source_rows, ((1,), (0,)))
        got = exchange_cores(sent)
        kept = product(own, source_rows, ((1,), (0,)))
        forward = scatter_sum(kept + got, CHIP)
        partial = product(own, own_rows, ((0,), (0,))) + product(other, other_rows, ((0,), (0,)))
        reverse = scatter_sum(partial, DST)
        weights, bias = layer_weights[layer], layer_biases[layer]
        row_block = mix(turn(forward), reverse, weights, bias)
        if layer + 1 < LAYERS:
            column_block = mix(forward, turn(reverse), weights, bias)
    return row_block


def solution(mesh):
    fine = Mesh(mesh.devices.reshape([SIZE[a] for a in SRC + DST]), SRC + DST)
    placed = (P(DST, SRC), P(SRC + DST, None), P(), P())
    return jax.shard_map(
        body, mesh=fine, in_specs=placed, out_specs=P(SRC + DST, None), check_vma=False
    )
```

```python
import itertools

import jax
import jax.numpy as jnp
from jax import lax
from jax.sharding import Mesh
from jax.sharding import PartitionSpec as P

LAYERS = 2

SRC = ("z", "xh", "core")
DST = ("xl", "y")
SIZE = {"z": 4, "xh": 2, "core": 2, "xl": 2, "y": 4}
PARTS = 8


def swap(value, axis, step):
    return lax.ppermute(value, axis, [(i, i ^ step) for i in range(SIZE[axis])])


def pair(block, axis):
    got = swap(block, axis, 1)
    first = lax.axis_index(axis) == 0
    return jnp.stack([jnp.where(first, block, got), jnp.where(first, got, block)])


def gather(block, short, ring):
    both = pair(block, short)
    me = lax.axis_index(ring)
    return [(me, both)] + [(me ^ step, swap(both, ring, step)) for step in (2, 1, 3)]


def gather_dst(block):
    rows, width = block.shape
    whole = jnp.zeros((2, 4, rows, width), block.dtype)
    for at, both in gather(block, "xl", "y"):
        whole = lax.dynamic_update_slice(whole, both[:, None], (0, at, 0, 0))
    return whole.reshape(-1, width)


def gather_chip(block):
    rows, width = block.shape
    whole = jnp.zeros((4, 2, rows, width), block.dtype)
    for at, both in gather(block, "xh", "z"):
        whole = lax.dynamic_update_slice(whole, both[None], (at, 0, 0, 0))
    return whole.reshape(-1, width)


def reduce_pair(both, axis):
    first = lax.axis_index(axis) == 0
    kept = jnp.where(first, both[0], both[1])
    return kept + swap(jnp.where(first, both[1], both[0]), axis, 1)


def reduce_dst(parts):
    parts = parts.reshape(2, 4, -1, parts.shape[1])
    me = lax.axis_index("y")
    share = lambda at: lax.dynamic_slice_in_dim(parts, at, 1, 1)[:, 0]
    got = [swap(share(me ^ step), "y", step) for step in (2, 1, 3)]
    return reduce_pair(share(me) + got[0] + got[1] + got[2], "xl")


def reduce_chip(parts):
    parts = parts.reshape(4, 2, -1, parts.shape[1])
    me = lax.axis_index("z")
    share = lambda at: lax.dynamic_slice_in_dim(parts, at, 1, 0)[0]
    got = [swap(share(me ^ step), "z", step) for step in (2, 1, 3)]
    return reduce_pair(share(me) + got[0] + got[1] + got[2], "xh")


def exchange_cores(value):
    return lax.ppermute(value, "core", [(0, 1), (1, 0)])


def turn(value):
    pairs = []
    for chip, core, dst in itertools.product(range(PARTS), range(2), range(PARTS)):
        pairs.append(((chip * 2 + core) * PARTS + dst, (dst * 2 + core) * PARTS + chip))
    return lax.ppermute(value, SRC + DST, pairs)


def split(value):
    high = lax.reduce_precision(value, 8, 7)
    return high.astype(jnp.bfloat16), (value - high).astype(jnp.bfloat16)


def product(left, right, dims):
    dot = lambda a, b: lax.dot_general(a, b, (dims, ((), ())), preferred_element_type=jnp.float32)
    return dot(left[0], right[0]) + dot(left[0], right[1]) + dot(left[1], right[0])


def mix(forward, reverse, weights, bias):
    dot = lambda a, b: jnp.dot(
        a, b, precision=lax.Precision.HIGHEST, preferred_element_type=jnp.float32
    )
    return jax.nn.relu(dot(forward, weights[0]) + dot(reverse, weights[1]) + bias[None, :])


def body(adjacency, features, layer_weights, layer_biases):
    core = lax.axis_index("core")
    half = adjacency.shape[0] // 2
    own = split(lax.dynamic_slice_in_dim(adjacency, core * half, half, 0))
    other = split(lax.dynamic_slice_in_dim(adjacency, (1 - core) * half, half, 0))
    row_block = features
    column_block = turn(features)
    for layer in range(LAYERS):
        source_rows = split(gather_dst(row_block))
        own_rows = gather_chip(column_block)
        other_rows = split(exchange_cores(own_rows))
        own_rows = split(own_rows)
        sent = product(other, source_rows, ((1,), (0,)))
        got = exchange_cores(sent)
        kept = product(own, source_rows, ((1,), (0,)))
        forward = reduce_chip(kept + got)
        partial = product(own, own_rows, ((0,), (0,))) + product(other, other_rows, ((0,), (0,)))
        reverse = reduce_dst(partial)
        weights, bias = layer_weights[layer], layer_biases[layer]
        row_block = mix(turn(forward), reverse, weights, bias)
        if layer + 1 < LAYERS:
            column_block = mix(forward, turn(reverse), weights, bias)
    return row_block


def solution(mesh):
    fine = Mesh(mesh.devices.reshape([SIZE[a] for a in SRC + DST]), SRC + DST)
    placed = (P(DST, SRC), P(SRC + DST, None), P(), P())
    return jax.shard_map(
        body, mesh=fine, in_specs=placed, out_specs=P(SRC + DST, None), check_vma=False
    )
```

```python
import itertools

import jax
import jax.numpy as jnp
from jax import lax
from jax.sharding import Mesh
from jax.sharding import PartitionSpec as P

LAYERS = 2

SRC = ("z", "xh", "core")
DST = ("xl", "y")
SIZE = {"z": 4, "xh": 2, "core": 2, "xl": 2, "y": 4}
PARTS = 8


def column_chip(block, share):
    high, middle, low = (share >> 2) & 1, (share >> 1) & 1, share & 1
    z = ((low ^ (block >> 1)) & 1) * 2 + (middle ^ (block >> 2))
    return z * 2 + (high ^ (block & 1))


def places(short):
    if short == "xl":
        return lax.axis_index("xl"), lambda at: at
    xl, y = lax.axis_index("xl"), lax.axis_index("y")
    return lax.axis_index("xh") ^ (y & 1), lambda at: ((at & 1) ^ xl) * 2 + ((at >> 1) ^ (y >> 1))


def swap(value, axis, step):
    return lax.ppermute(value, axis, [(i, i ^ step) for i in range(SIZE[axis])])


def gather(block, short, ring):
    rows, width = block.shape
    me = lax.axis_index(ring)
    in_pair, place = places(short)
    got = swap(block, short, 1)
    first = in_pair == 0
    both = jnp.stack([jnp.where(first, block, got), jnp.where(first, got, block)])
    whole = jnp.zeros((2, 4, rows, width), block.dtype)
    whole = lax.dynamic_update_slice(whole, both[:, None], (0, place(me), 0, 0))
    for step in (2, 1, 3):
        got = swap(both, ring, step)
        whole = lax.dynamic_update_slice(whole, got[:, None], (0, place(me ^ step), 0, 0))
    return whole.reshape(-1, width)


def reduce(parts, short, ring):
    parts = parts.reshape(2, 4, -1, parts.shape[1])
    me = lax.axis_index(ring)
    in_pair, place = places(short)
    share = lambda at: lax.dynamic_slice_in_dim(parts, place(at), 1, 1)[:, 0]
    got = [swap(share(me ^ step), ring, step) for step in (2, 1, 3)]
    both = share(me) + got[0] + got[1] + got[2]
    first = in_pair == 0
    sent = swap(jnp.where(first, both[1], both[0]), short, 1)
    return jnp.where(first, both[0], both[1]) + sent


def exchange_cores(value):
    return lax.ppermute(value, "core", [(0, 1), (1, 0)])


def turn(value, to_rows):
    pairs = []
    for block, core, share in itertools.product(range(PARTS), range(2), range(PARTS)):
        row = (block * 2 + core) * PARTS + share
        column = (column_chip(block, share) * 2 + core) * PARTS + block
        pairs.append((column, row) if to_rows else (row, column))
    return lax.ppermute(value, SRC + DST, pairs)


def split(value):
    high = lax.reduce_precision(value, 8, 7)
    return high.astype(jnp.bfloat16), (value - high).astype(jnp.bfloat16)


def product(left, right, dims):
    dot = lambda a, b: lax.dot_general(a, b, (dims, ((), ())), preferred_element_type=jnp.float32)
    width = right[0].shape[1]
    wide = dot(left[0], jnp.concatenate(right, axis=1))
    return wide[:, :width] + wide[:, width:] + dot(left[1], right[0])


def mix(forward, reverse, weights, bias):
    both = split(jnp.concatenate([forward, reverse], axis=1))
    stacked = split(weights.reshape(-1, weights.shape[-1]))
    return jax.nn.relu(product(both, stacked, ((1,), (0,))) + bias[None, :])


def body(adjacency, features, layer_weights, layer_biases):
    core = lax.axis_index("core")
    half = adjacency.shape[0] // 2
    row_block = features
    for layer in range(LAYERS):
        if layer == 0:
            column_block = turn(features, False)
            own = split(lax.dynamic_slice_in_dim(adjacency, core * half, half, 0))
            other = split(lax.dynamic_slice_in_dim(adjacency, (1 - core) * half, half, 0))
        source_rows = split(gather(row_block, "xl", "y"))
        own_rows = gather(column_block, "xh", "z")
        other_rows = exchange_cores(own_rows)
        other_rows = split(other_rows)
        own_rows = split(own_rows)
        sent = product(other, source_rows, ((1,), (0,)))
        got = exchange_cores(sent)
        kept = product(own, source_rows, ((1,), (0,)))
        forward = reduce(kept + got, "xh", "z")
        partial = product(own, own_rows, ((0,), (0,)))
        partial = partial + product(other, other_rows, ((0,), (0,)))
        reverse = reduce(partial, "xl", "y")
        weights, bias = layer_weights[layer], layer_biases[layer]
        turned_forward = turn(forward, True)
        row_block = mix(turned_forward, reverse, weights, bias)
        if layer + 1 < LAYERS:
            turned_reverse = turn(reverse, False)
            column_block = mix(forward, turned_reverse, weights, bias)
    return row_block


def solution(mesh):
    fine = Mesh(mesh.devices.reshape([SIZE[a] for a in SRC + DST]), SRC + DST)
    placed = (P(DST, SRC), P(SRC + DST, None), P(), P())
    return jax.shard_map(
        body, mesh=fine, in_specs=placed, out_specs=P(SRC + DST, None), check_vma=False
    )
```

```python
import itertools

import jax
import jax.numpy as jnp
from jax import lax
from jax.sharding import Mesh
from jax.sharding import PartitionSpec as P

LAYERS = 2

SRC = ("z", "xh", "core")
DST = ("xl", "y")
SIZE = {"z": 4, "xh": 2, "core": 2, "xl": 2, "y": 4}
PARTS = 8


def column_chip(block, share):
    high, middle, low = (share >> 2) & 1, (share >> 1) & 1, share & 1
    z = ((low ^ (block >> 1)) & 1) * 2 + (middle ^ (block >> 2))
    return z * 2 + (high ^ (block & 1))


def places(short):
    if short == "xl":
        return lax.axis_index("xl"), lambda at: at
    xl, y = lax.axis_index("xl"), lax.axis_index("y")
    return lax.axis_index("xh") ^ (y & 1), lambda at: ((at & 1) ^ xl) * 2 + ((at >> 1) ^ (y >> 1))


def swap(value, axis, step):
    return lax.ppermute(value, axis, [(i, i ^ step) for i in range(SIZE[axis])])


def gather(block, short, ring, got=None):
    rows, width = block.shape
    me = lax.axis_index(ring)
    in_pair, place = places(short)
    if got is None:
        got = swap(block, short, 1)
    first = in_pair == 0
    both = jnp.stack([jnp.where(first, block, got), jnp.where(first, got, block)])
    whole = jnp.zeros((2, 4, rows, width), block.dtype)
    whole = lax.dynamic_update_slice(whole, both[:, None], (0, place(me), 0, 0))
    for step in (2, 1, 3):
        got = swap(both, ring, step)
        whole = lax.dynamic_update_slice(whole, got[:, None], (0, place(me ^ step), 0, 0))
    return whole.reshape(-1, width)


def reduce(parts, short, ring):
    parts = parts.reshape(2, 4, -1, parts.shape[1])
    me = lax.axis_index(ring)
    in_pair, place = places(short)
    share = lambda at: lax.dynamic_slice_in_dim(parts, place(at), 1, 1)[:, 0]
    got = [swap(share(me ^ step), ring, step) for step in (2, 1, 3)]
    both = share(me) + got[0] + got[1] + got[2]
    first = in_pair == 0
    sent = swap(jnp.where(first, both[1], both[0]), short, 1)
    return jnp.where(first, both[0], both[1]) + sent


def reduce_to_rows(parts, ring):
    parts = parts.reshape(2, 4, -1, parts.shape[1])
    me = lax.axis_index(ring)
    in_pair, place = places("xh")
    share = lambda at: lax.dynamic_slice_in_dim(parts, place(at), 1, 1)[:, 0]
    got = [swap(share(me ^ step), ring, step) for step in (2, 1, 3)]
    both = share(me) + got[0] + got[1] + got[2]
    first = in_pair == 0
    own = turn(jnp.where(first, both[0], both[1]), True)
    return own + turn(jnp.where(first, both[1], both[0]), True, 1)


def exchange_cores(value):
    return lax.ppermute(value, "core", [(0, 1), (1, 0)])


def turn(value, to_rows, flip=0):
    pairs = []
    for block, core, share in itertools.product(range(PARTS), range(2), range(PARTS)):
        row = (block * 2 + core) * PARTS + share
        column = ((column_chip(block, share) ^ flip) * 2 + core) * PARTS + block
        pairs.append((column, row) if to_rows else (row, column))
    return lax.ppermute(value, SRC + DST, pairs)


def split(value):
    high = lax.reduce_precision(value, 8, 7)
    return high.astype(jnp.bfloat16), (value - high).astype(jnp.bfloat16)


def product(left, right, dims):
    dot = lambda a, b: lax.dot_general(a, b, (dims, ((), ())), preferred_element_type=jnp.float32)
    width = right[0].shape[1]
    wide = dot(left[0], jnp.concatenate(right, axis=1))
    return wide[:, :width] + wide[:, width:] + dot(left[1], right[0])


def mix(forward, reverse, weights, bias):
    both = split(jnp.concatenate([forward, reverse], axis=1))
    stacked = split(weights.reshape(-1, weights.shape[-1]))
    return jax.nn.relu(product(both, stacked, ((1,), (0,))) + bias[None, :])


def body(adjacency, features, layer_weights, layer_biases):
    core = lax.axis_index("core")
    half = adjacency.shape[0] // 2
    row_block = features
    for layer in range(LAYERS):
        if layer == 0:
            column_block = turn(features, False)
            own = split(lax.dynamic_slice_in_dim(adjacency, core * half, half, 0))
            other = split(lax.dynamic_slice_in_dim(adjacency, (1 - core) * half, half, 0))
        source_rows = split(gather(row_block, "xl", "y"))
        own_rows = gather(column_block, "xh", "z")
        other_rows = exchange_cores(own_rows)
        other_rows = split(other_rows)
        own_rows = split(own_rows)
        sent = product(other, source_rows, ((1,), (0,)))
        got = exchange_cores(sent)
        kept = product(own, source_rows, ((1,), (0,)))
        last = layer + 1 == LAYERS
        if last:
            turned_forward = reduce_to_rows(kept + got, "z")
        else:
            forward = reduce(kept + got, "xh", "z")
            turned_forward = turn(forward, True)
        partial = product(own, own_rows, ((0,), (0,)))
        partial = partial + product(other, other_rows, ((0,), (0,)))
        reverse = reduce(partial, "xl", "y")
        weights, bias = layer_weights[layer], layer_biases[layer]
        row_block = mix(turned_forward, reverse, weights, bias)
        if not last:
            turned_reverse = turn(reverse, False)
            column_block = mix(forward, turned_reverse, weights, bias)
    return row_block


def solution(mesh):
    fine = Mesh(mesh.devices.reshape([SIZE[a] for a in SRC + DST]), SRC + DST)
    placed = (P(DST, SRC), P(SRC + DST, None), P(), P())
    return jax.shard_map(
        body, mesh=fine, in_specs=placed, out_specs=P(SRC + DST, None), check_vma=False
    )
```

```python
import itertools

import jax
import jax.numpy as jnp
from jax import lax
from jax.sharding import Mesh
from jax.sharding import PartitionSpec as P

LAYERS = 2

SRC = ("z", "xh", "core")
DST = ("xl", "y")
SIZE = {"z": 4, "xh": 2, "core": 2, "xl": 2, "y": 4}
PARTS = 8


def column_chip(block, share):
    high, middle, low = (share >> 2) & 1, (share >> 1) & 1, share & 1
    z = ((low ^ (block >> 1)) & 1) * 2 + (middle ^ (block >> 2))
    return z * 2 + (high ^ (block & 1))


def places(short):
    if short == "xl":
        return lax.axis_index("xl"), lambda at: at
    xl, y = lax.axis_index("xl"), lax.axis_index("y")
    return lax.axis_index("xh") ^ (y & 1), lambda at: ((at & 1) ^ xl) * 2 + ((at >> 1) ^ (y >> 1))


def swap(value, axis, step):
    return lax.ppermute(value, axis, [(i, i ^ step) for i in range(SIZE[axis])])


def gather(block, short, ring, got=None):
    rows, width = block.shape
    me = lax.axis_index(ring)
    in_pair, place = places(short)
    if got is None:
        got = swap(block, short, 1)
    first = in_pair == 0
    both = jnp.stack([jnp.where(first, block, got), jnp.where(first, got, block)])
    whole = jnp.zeros((2, 4, rows, width), block.dtype)
    whole = lax.dynamic_update_slice(whole, both[:, None], (0, place(me), 0, 0))
    for step in (1, 3, 2):
        got = swap(both, ring, step)
        whole = lax.dynamic_update_slice(whole, got[:, None], (0, place(me ^ step), 0, 0))
    return whole.reshape(-1, width)


def reduce(parts, short, ring):
    parts = parts.reshape(2, 4, -1, parts.shape[1])
    me = lax.axis_index(ring)
    in_pair, place = places(short)
    share = lambda at: lax.dynamic_slice_in_dim(parts, place(at), 1, 1)[:, 0]
    got = [swap(share(me ^ step), ring, step) for step in (2, 1, 3)]
    both = share(me) + got[0] + got[1] + got[2]
    first = in_pair == 0
    sent = swap(jnp.where(first, both[1], both[0]), short, 1)
    return jnp.where(first, both[0], both[1]) + sent


def reduce_to_rows(parts, ring):
    parts = parts.reshape(2, 4, -1, parts.shape[1])
    me = lax.axis_index(ring)
    in_pair, place = places("xh")
    share = lambda at: lax.dynamic_slice_in_dim(parts, place(at), 1, 1)[:, 0]
    got = [swap(share(me ^ step), ring, step) for step in (2, 1, 3)]
    both = share(me) + got[0] + got[1] + got[2]
    first = in_pair == 0
    own = turn(jnp.where(first, both[0], both[1]), True)
    return own + turn(jnp.where(first, both[1], both[0]), True, 1)


def exchange_cores(value):
    return lax.ppermute(value, "core", [(0, 1), (1, 0)])


def turn(value, to_rows, flip=0):
    pairs = []
    for block, core, share in itertools.product(range(PARTS), range(2), range(PARTS)):
        row = (block * 2 + core) * PARTS + share
        column = ((column_chip(block, share) ^ flip) * 2 + core) * PARTS + block
        pairs.append((column, row) if to_rows else (row, column))
    return lax.ppermute(value, SRC + DST, pairs)


def split(value):
    high = lax.reduce_precision(value, 8, 7)
    return high.astype(jnp.bfloat16), (value - high).astype(jnp.bfloat16)


def product(left, right, dims):
    dot = lambda a, b: lax.dot_general(a, b, (dims, ((), ())), preferred_element_type=jnp.float32)
    width = right[0].shape[1]
    wide = dot(left[0], jnp.concatenate(right, axis=1))
    return wide[:, :width] + wide[:, width:] + dot(left[1], right[0])


def mix(forward, reverse, weights, bias):
    both = split(jnp.concatenate([forward, reverse], axis=1))
    return jax.nn.relu(product(both, weights, ((1,), (0,))) + bias[None, :])


def body(adjacency, features, layer_weights, layer_biases):
    core = lax.axis_index("core")
    half = adjacency.shape[0] // 2
    row_block = features
    for layer in range(LAYERS):
        if layer == 0:
            column_block = turn(features, False)
            stacked = split(layer_weights.reshape(LAYERS, -1, layer_weights.shape[-1]))
            own = split(lax.dynamic_slice_in_dim(adjacency, core * half, half, 0))
            other = split(lax.dynamic_slice_in_dim(adjacency, (1 - core) * half, half, 0))
        source_rows = split(gather(row_block, "xl", "y"))
        own_rows = gather(column_block, "xh", "z")
        other_rows = exchange_cores(own_rows)
        other_rows = split(other_rows)
        own_rows = split(own_rows)
        sent = product(other, source_rows, ((1,), (0,)))
        got = exchange_cores(sent)
        kept = product(own, source_rows, ((1,), (0,)))
        last = layer + 1 == LAYERS
        if last:
            turned_forward = reduce_to_rows(kept + got, "z")
        else:
            forward = reduce(kept + got, "xh", "z")
            turned_forward = turn(forward, True)
        partial = product(own, own_rows, ((0,), (0,)))
        partial = partial + product(other, other_rows, ((0,), (0,)))
        reverse = reduce(partial, "xl", "y")
        weights, bias = [half[layer] for half in stacked], layer_biases[layer]
        row_block = mix(turned_forward, reverse, weights, bias)
        if not last:
            turned_reverse = turn(reverse, False)
            column_block = mix(forward, turned_reverse, weights, bias)
    return row_block


def solution(mesh):
    fine = Mesh(mesh.devices.reshape([SIZE[a] for a in SRC + DST]), SRC + DST)
    placed = (P(DST, SRC), P(SRC + DST, None), P(), P())
    return jax.shard_map(
        body, mesh=fine, in_specs=placed, out_specs=P(SRC + DST, None), check_vma=False
    )
```

```python
import itertools

import jax
import jax.numpy as jnp
from jax import lax
from jax.sharding import Mesh
from jax.sharding import PartitionSpec as P

LAYERS = 2

SRC = ("z", "xh", "core")
DST = ("xl", "y")
SIZE = {"z": 4, "xh": 2, "core": 2, "xl": 2, "y": 4}
PARTS = 8


def column_chip(block, share):
    high, middle, low = (share >> 2) & 1, (share >> 1) & 1, share & 1
    z = ((low ^ (block >> 1)) & 1) * 2 + (middle ^ (block >> 2))
    return z * 2 + (high ^ (block & 1))


def places(short):
    if short == "xl":
        return lax.axis_index("xl"), lambda at: at
    xl, y = lax.axis_index("xl"), lax.axis_index("y")
    return lax.axis_index("xh") ^ (y & 1), lambda at: ((at & 1) ^ xl) * 2 + ((at >> 1) ^ (y >> 1))


def swap(value, axis, step):
    return lax.ppermute(value, axis, [(i, i ^ step) for i in range(SIZE[axis])])


def gather(block, short, ring, name, got=None):
    rows, width = block.shape
    me = lax.axis_index(ring)
    in_pair, place = places(short)
    if got is None:
        got = swap(block, short, 1)
    first = in_pair == 0
    both = jnp.stack([jnp.where(first, block, got), jnp.where(first, got, block)])
    whole = jnp.zeros((2, 4, rows, width), block.dtype)
    whole = lax.dynamic_update_slice(whole, both[:, None], (0, place(me), 0, 0))
    for step in ((1, 3, 2) if name == "row" else (2, 1, 3)):
        got = swap(both, ring, step)
        whole = lax.dynamic_update_slice(whole, got[:, None], (0, place(me ^ step), 0, 0))
    return whole.reshape(-1, width)


def reduce(parts, short, ring):
    parts = parts.reshape(2, 4, -1, parts.shape[1])
    me = lax.axis_index(ring)
    in_pair, place = places(short)
    share = lambda at: lax.dynamic_slice_in_dim(parts, place(at), 1, 1)[:, 0]
    got = [swap(share(me ^ step), ring, step) for step in (2, 1, 3)]
    both = share(me) + got[0] + got[1] + got[2]
    first = in_pair == 0
    sent = swap(jnp.where(first, both[1], both[0]), short, 1)
    return jnp.where(first, both[0], both[1]) + sent


def reduce_to_rows(parts, ring):
    parts = parts.reshape(2, 4, -1, parts.shape[1])
    me = lax.axis_index(ring)
    in_pair, place = places("xh")
    share = lambda at: lax.dynamic_slice_in_dim(parts, place(at), 1, 1)[:, 0]
    got = [swap(share(me ^ step), ring, step) for step in (2, 1, 3)]
    both = share(me) + got[0] + got[1] + got[2]
    first = in_pair == 0
    own = turn(jnp.where(first, both[0], both[1]), True)
    return own + turn(jnp.where(first, both[1], both[0]), True, 1)


def exchange_cores(value):
    return lax.ppermute(value, "core", [(0, 1), (1, 0)])


def turn(value, to_rows, flip=0):
    pairs = []
    for block, core, share in itertools.product(range(PARTS), range(2), range(PARTS)):
        row = (block * 2 + core) * PARTS + share
        column = ((column_chip(block, share) ^ flip) * 2 + core) * PARTS + block
        pairs.append((column, row) if to_rows else (row, column))
    return lax.ppermute(value, SRC + DST, pairs)


def split(value):
    high = lax.reduce_precision(value, 8, 7)
    return high.astype(jnp.bfloat16), (value - high).astype(jnp.bfloat16)


def product(left, right, dims):
    dot = lambda a, b: lax.dot_general(a, b, (dims, ((), ())), preferred_element_type=jnp.float32)
    width = right[0].shape[1]
    wide = dot(left[0], jnp.concatenate(right, axis=1))
    return wide[:, :width] + wide[:, width:] + dot(left[1], right[0])


def mix(forward, reverse, weights, bias):
    both = split(jnp.concatenate([forward, reverse], axis=1))
    return jax.nn.relu(product(both, weights, ((1,), (0,))) + bias[None, :])


def body(adjacency, features, layer_weights, layer_biases):
    core = lax.axis_index("core")
    half = adjacency.shape[0] // 2
    row_block = features
    for layer in range(LAYERS):
        if layer == 0:
            column_block = turn(features, False)
            stacked = split(layer_weights.reshape(LAYERS, -1, layer_weights.shape[-1]))
            own = split(lax.dynamic_slice_in_dim(adjacency, core * half, half, 0))
            other = split(lax.dynamic_slice_in_dim(adjacency, (1 - core) * half, half, 0))
        source_rows = split(gather(row_block, "xl", "y", "row"))
        own_rows = gather(column_block, "xh", "z", "column")
        other_rows = exchange_cores(own_rows)
        other_rows = split(other_rows)
        own_rows = split(own_rows)
        sent = product(other, source_rows, ((1,), (0,)))
        got = exchange_cores(sent)
        kept = product(own, source_rows, ((1,), (0,)))
        last = layer + 1 == LAYERS
        if last:
            turned_forward = reduce_to_rows(kept + got, "z")
        else:
            forward = reduce(kept + got, "xh", "z")
            turned_forward = turn(forward, True)
        partial = product(own, own_rows, ((0,), (0,)))
        partial = partial + product(other, other_rows, ((0,), (0,)))
        reverse = reduce(partial, "xl", "y")
        weights, bias = [half[layer] for half in stacked], layer_biases[layer]
        row_block = mix(turned_forward, reverse, weights, bias)
        if not last:
            turned_reverse = turn(reverse, False)
            column_block = mix(forward, turned_reverse, weights, bias)
    return row_block


def solution(mesh):
    fine = Mesh(mesh.devices.reshape([SIZE[a] for a in SRC + DST]), SRC + DST)
    placed = (P(DST, SRC), P(SRC + DST, None), P(), P())
    return jax.shard_map(
        body, mesh=fine, in_specs=placed, out_specs=P(SRC + DST, None), check_vma=False
    )
```
